256 devices in a mesh: node: 16 (over z, core), head: 16 (over x, y).
Axes of the slice: x: 4, y: 4, z: 8, core: 2. Of those that a mesh axis runs over, the one named last changes fastest.
Arguments:
- features: bfloat16 [65536, 1024], P(('node', 'head')), may hold values from -6 to 6
- attn_gain: float32 [1024], replicated, may hold values from 0.25 to 1.75
- qkv_weight: bfloat16 [1024, 16, 192], P(None, 'head')
- out_weight: bfloat16 [1024, 1024], replicated, may hold values from -0.1875 to 0.1875
- feedforward_norm_gain: float32 [1024], replicated, may hold values from 0.25 to 1.75
- up_weight: bfloat16 [1024, 2048], replicated, may hold values from -0.1875 to 0.1875
- down_weight: bfloat16 [2048, 1024], replicated, may hold values from -0.125 to 0.125
- tile_pattern: int32 [512, 8], P('node'), may hold values from 0 to 511, as said below
- node_order: int32 [16, 4096], P('node'), may hold values from 0 to 4095, each once within a row
Outputs:
- updated: bfloat16 [65536, 1024], P(('node', 'head'))
The draws below stay inside these ranges and needn't reach their ends.
Inputs may be any that keep to these rules, and one draw needn't show every extreme that they name: `tile_pattern`: row t names 8 different tiles; the first is t itself; all lie in partitions (tiles p * 32 to (p + 1) * 32 - 1) at cyclic distance at most 2 from t's partition; the second lies 2 partitions below t's and the third 2 above. `node_order`: each row lists every local row of its partition once.
All inputs are finite; a program needn't handle non-finite values.
Results may differ from the reference program's by a relative error of at most 0.0045.
Values may be sent and summed in bfloat16 or wider, within the bound.
A program may use at most 64 MiB of HBM per device.

```python
import math
import jax
import jax.numpy as jnp
from jax import lax

D = 1024
HEADS = 16
HD = 64
FF = 2048
TILE = 128
NNZ = 8
REACH = 2
PARTS_SIZE = 16
ROWS_PART = 4096
QT = 32
NODES = 65536
NTILES = 512


def draw_features(key, part):
    noise_part = jax.random.normal(jax.random.fold_in(key, 1), (NODES, D), jnp.float32)
    return jnp.clip(noise_part, -6.0, 6.0).astype(jnp.bfloat16)


def draw_qkv_weight(key, part):
    base_draw = jax.random.normal(jax.random.fold_in(key, 1), (D, HEADS, 3 * HD), jnp.float32) * D ** (-0.5)
    return base_draw.astype(jnp.bfloat16)


def draw_tile_pattern(key, part):
    window = (2 * REACH + 1) * QT
    tiles = jnp.arange(NTILES, dtype=jnp.int32)
    partition = tiles // QT
    local_tile = tiles % QT
    candidate = jnp.arange(window, dtype=jnp.int32)[None, :]
    raw_scores = jax.random.randint(jax.random.fold_in(key, 1), (NTILES, window), 0, 65536, jnp.int32)
    raw_scores = raw_scores * window + candidate + 3
    own_slot = (REACH * QT + local_tile)[:, None]
    lower_position = jax.random.randint(jax.random.fold_in(key, 2), (NTILES, 1), 0, QT, jnp.int32)
    high_slot = 2 * REACH * QT + jax.random.randint(jax.random.fold_in(key, 3), (NTILES, 1), 0, QT, jnp.int32)
    raw_scores = jnp.where(candidate == own_slot, 0, jnp.where(candidate == lower_position, 1, jnp.where(candidate == high_slot, 2, raw_scores)))
    chosen = jnp.argsort(raw_scores, axis=1, stable=True)[:, :NNZ].astype(jnp.int32)
    target_part = (partition[:, None] - REACH + chosen // QT + PARTS_SIZE) % PARTS_SIZE
    return (target_part * QT + chosen % QT).astype(jnp.int32)


def noise(key, shape, deviation, limit, held_as=jnp.bfloat16):
    entries = deviation * jax.random.normal(key, shape, jnp.float32)
    return jnp.clip(entries, min=-limit, max=limit).astype(held_as)


def setup_inputs(seed: int = 0) -> dict:
    arg_keys = jax.random.split(jax.random.key(seed), 10)
    features = draw_features(jax.random.fold_in(arg_keys[9], 71), 0)
    attn_gain = jnp.clip(1.0 + 0.15 * jax.random.normal(arg_keys[1], (D,), jnp.float32), 0.25, 1.75)
    qkv_weight = draw_qkv_weight(jax.random.fold_in(arg_keys[9], 71), 0)
    out_weight = noise(arg_keys[3], (D, D), D ** -0.5, 0.1875)
    feedforward_norm_gain = jnp.clip(1.0 + 0.15 * jax.random.normal(arg_keys[4], (D,), jnp.float32), 0.25, 1.75)
    up_weight = noise(arg_keys[5], (D, FF), D ** -0.5, 0.1875)
    down_weight = noise(arg_keys[6], (FF, D), FF ** -0.5, 0.125)
    tile_pattern = draw_tile_pattern(jax.random.fold_in(arg_keys[9], 71), 0)
    node_order = jax.vmap(lambda own: jax.random.permutation(own, ROWS_PART))(jax.random.split(arg_keys[8], PARTS_SIZE)).reshape((PARTS_SIZE, ROWS_PART)).astype(jnp.int32)
    return {"features": features, "attn_gain": attn_gain, "qkv_weight": qkv_weight, "out_weight": out_weight, "feedforward_norm_gain": feedforward_norm_gain, "up_weight": up_weight, "down_weight": down_weight, "tile_pattern": tile_pattern, "node_order": node_order}


def layer_norm(values, gain):
    row_mean = lax.optimization_barrier(jnp.mean(values, -1, keepdims=True))
    centred = values - row_mean
    variance = lax.optimization_barrier(jnp.mean(centred * centred, -1, keepdims=True))
    return centred * lax.rsqrt(variance + 1e-05) * gain.astype(jnp.float32)

def reference(features, attn_gain, qkv_weight, out_weight, feedforward_norm_gain, up_weight, down_weight, tile_pattern, node_order):
    flattened_weight = qkv_weight.reshape(D, HEADS * 3 * HD)
    score_scale = 1.0 / math.sqrt(HD)

    def project(row_block):
        normed = layer_norm(row_block.astype(jnp.float32), attn_gain).astype(jnp.bfloat16)
        return jnp.dot(normed, flattened_weight, preferred_element_type=jnp.float32).astype(jnp.bfloat16)
    projected = lax.map(project, features.reshape(PARTS_SIZE, ROWS_PART, D))
    projected = projected.reshape(PARTS_SIZE, ROWS_PART, HEADS, 3 * HD)
    cluster = jax.vmap(lambda row_block, partition_permutation: row_block[partition_permutation])(projected, node_order)
    queries = cluster[..., :HD].reshape(NTILES, TILE, HEADS, HD)
    keyval = cluster[..., HD:].reshape(NTILES, TILE, HEADS, 2 * HD)

    def attend(item_pair):
        tile_queries, columns = item_pair
        picked = keyval[columns]
        key_tiles = picked[..., :HD].astype(jnp.float32)
        value_tile_blocks = picked[..., HD:].reshape(NNZ * TILE, HEADS, HD).astype(jnp.float32)
        scores = jnp.einsum('qhd,nkhd->hqnk', tile_queries.astype(jnp.float32), key_tiles)
        scores = scores.reshape(HEADS, TILE, NNZ * TILE) * score_scale
        row_max = lax.optimization_barrier(jnp.max(scores, -1, keepdims=True))
        expd = jnp.exp(scores - row_max)
        weight_arrays = (expd / lax.optimization_barrier(jnp.sum(expd, -1, keepdims=True))).astype(jnp.bfloat16)
        return jnp.einsum('jzc,cju->zju', weight_arrays.astype(jnp.float32), value_tile_blocks).astype(jnp.bfloat16)
    attended = lax.map(attend, (queries, tile_pattern)).reshape(PARTS_SIZE, ROWS_PART, HEADS * HD)
    restored = jax.vmap(lambda row_block, partition_permutation: jnp.zeros_like(row_block).at[partition_permutation].set(row_block))(attended, node_order)

    def finish(item_pair):
        rows_in, attn_rows = item_pair
        residual = rows_in.astype(jnp.float32) + jnp.dot(attn_rows, out_weight, preferred_element_type=jnp.float32)
        mlp_input = layer_norm(residual, feedforward_norm_gain).astype(jnp.bfloat16)
        hidden = jax.nn.gelu(jnp.dot(mlp_input, up_weight, preferred_element_type=jnp.float32)).astype(jnp.bfloat16)
        return (residual + jnp.dot(hidden, down_weight, preferred_element_type=jnp.float32)).astype(jnp.bfloat16)
    updated = lax.map(finish, (features.reshape(PARTS_SIZE, ROWS_PART, D), restored))
    return updated.reshape(NODES, D)
```

```python
import math

import jax
import jax.numpy as jnp
from jax import lax
from jax.experimental import pallas as pl
from jax.experimental.pallas import tpu as pltpu
from jax.sharding import PartitionSpec as P

D = 1024
HD = 64
TILE = 128
NNZ = 8
REACH = 2
WINDOW = 2 * REACH + 1
UNROLL = 16


def passed_along(x, axis, by):
    size = lax.axis_size(axis)
    return lax.ppermute(x, axis, [(i, (i + by) % size) for i in range(size)])


def layer_norm(values, gain):
    row_mean = jnp.mean(values, -1, keepdims=True)
    centred = values - row_mean
    variance = jnp.mean(centred * centred, -1, keepdims=True)
    return centred * lax.rsqrt(variance + 1e-05) * gain


def reorder_kernel(order_ref, rows_ref, keyval_ref, query_ref, src_kv, src_q, dst_kv, dst_q):
    rows = rows_ref.shape[0]

    @pl.loop(0, rows // 128)
    def _(b):
        at = pl.ds(pl.multiple_of(b * 128, 128), 128)
        src_kv[at, :] = rows_ref[at, :128].astype(jnp.float32)
        src_q[at, :] = rows_ref[at, 128:].astype(jnp.float32)

    @pl.loop(0, rows // UNROLL)
    def _(b):
        base = pl.multiple_of(b * UNROLL, UNROLL)
        for r in range(UNROLL):
            at = order_ref[base + r]
            dst_kv[pl.ds(base + r, 1), :] = src_kv[pl.ds(at, 1), :]
            dst_q[pl.ds(base + r, 1), :] = src_q[pl.ds(at, 1), :]

    @pl.loop(0, rows // 128)
    def _(b):
        at = pl.ds(pl.multiple_of(b * 128, 128), 128)
        keyval_ref[at, :] = dst_kv[at, :].astype(jnp.bfloat16)
        query_ref[at, :] = dst_q[at, :].astype(jnp.bfloat16)


def reorder(order, rows):
    n = rows.shape[0]
    vmem = pl.BlockSpec(memory_space=pltpu.VMEM)
    return pl.pallas_call(
        reorder_kernel,
        out_shape=[jax.ShapeDtypeStruct((n, 2 * HD), jnp.bfloat16)] * 2,
        in_specs=[pl.BlockSpec(memory_space=pltpu.SMEM), vmem],
        out_specs=[vmem, vmem],
        scratch_shapes=[pltpu.VMEM((n, 2 * HD), jnp.float32)] * 4,
        compiler_params=pltpu.CompilerParams(vmem_limit_bytes=40 << 20),
        name="reorder",
    )(order, rows)


def attend_tile(t, position_ref, order_ref, query_ref, window, tile_out, restored):
    scale = math.log2(math.e) / math.sqrt(HD)
    query = query_ref[pl.ds(pl.multiple_of(t * TILE, TILE), TILE), :]
    keyval = jnp.concatenate([window[position_ref[t, n]] for n in range(NNZ)], axis=0)
    scores = lax.dot_general(
        query, keyval, (((1,), (1,)), ((), ())), preferred_element_type=jnp.float32
    )
    scores = scores * scale
    expd = jnp.exp2(scores - jnp.max(scores, -1, keepdims=True))
    total = jnp.sum(expd, -1, keepdims=True)
    mixed = jnp.dot(expd.astype(jnp.bfloat16), keyval, preferred_element_type=jnp.float32)
    tile_out[...] = mixed / total
    for r in range(TILE):
        restored[pl.ds(order_ref[t * TILE + r], 1), :] = tile_out[pl.ds(r, 1), :]


def attention_kernel(
    position_ref, order_ref, query_ref, b0, b1, b2, b3, b4, out_ref, window, tile_out, restored, sems
):
    tiles = query_ref.shape[0] // TILE
    copies = []
    for k, block in enumerate((b0, b1, b2, b3, b4)):
        copy = pltpu.make_async_copy(block, window.at[pl.ds(k * tiles, tiles)], sems.at[k])
        copy.start()
        copies.append(copy)
    for copy in copies:
        copy.wait()

    @pl.loop(0, tiles)
    def _(t):
        attend_tile(t, position_ref, order_ref, query_ref, window, tile_out, restored)

    @pl.loop(0, tiles)
    def _(t):
        at = pl.ds(pl.multiple_of(t * TILE, TILE), TILE)
        out_ref[at, :] = restored[at, HD:].astype(jnp.bfloat16)


def attention(position, order, query, blocks):
    n = query.shape[0]
    tiles = n // TILE
    smem = pl.BlockSpec(memory_space=pltpu.SMEM)
    vmem = pl.BlockSpec(memory_space=pltpu.VMEM)
    hbm = pl.BlockSpec(memory_space=pl.ANY)
    return pl.pallas_call(
        attention_kernel,
        out_shape=jax.ShapeDtypeStruct((n, HD), jnp.bfloat16),
        in_specs=[smem, smem, vmem] + [hbm] * WINDOW,
        out_specs=vmem,
        scratch_shapes=[
            pltpu.VMEM((WINDOW * tiles, TILE, 2 * HD), jnp.bfloat16),
            pltpu.VMEM((TILE, 2 * HD), jnp.float32),
            pltpu.VMEM((n, 2 * HD), jnp.float32),
            pltpu.SemaphoreType.DMA((WINDOW,)),
        ],
        compiler_params=pltpu.CompilerParams(vmem_limit_bytes=40 << 20),
        name="attention",
    )(position, order, query, *[b.reshape(tiles, TILE, 2 * HD) for b in blocks])


def shards(
    features,
    attn_gain,
    qkv_weight,
    out_weight,
    feedforward_norm_gain,
    up_weight,
    down_weight,
    tile_pattern,
    node_order,
):
    own_rows = features.shape[0]
    partitions = lax.axis_size("node")
    rows_part = own_rows * lax.axis_size("head")
    query_tiles = rows_part // TILE
    normed = layer_norm(features.astype(jnp.float32), attn_gain).astype(jnp.bfloat16)
    weight = qkv_weight[:, 0]
    weight = jnp.concatenate(
        [weight[:, HD:], weight[:, :HD], jnp.zeros((D, HD), jnp.bfloat16)], -1
    )
    projected = jnp.dot(
        lax.all_gather(normed, "head", axis=0, tiled=True),
        weight,
        preferred_element_type=jnp.float32,
    ).astype(jnp.bfloat16)
    order = node_order[0]
    keyval, query = reorder(order, projected)
    blocks = [
        keyval if by == 0 else passed_along(keyval, "node", -by)
        for by in range(-REACH, REACH + 1)
    ]
    partition = lax.axis_index("node")
    position = (
        tile_pattern // query_tiles - partition + REACH + partitions
    ) % partitions * query_tiles + tile_pattern % query_tiles
    restored = attention(position, order, query, blocks)
    gathered_heads = lax.all_to_all(restored, "head", split_axis=0, concat_axis=1, tiled=True)
    residual = features.astype(jnp.float32) + jnp.dot(
        gathered_heads, out_weight, preferred_element_type=jnp.float32
    )
    mlp_input = layer_norm(residual, feedforward_norm_gain).astype(jnp.bfloat16)
    hidden = jax.nn.gelu(jnp.dot(mlp_input, up_weight, preferred_element_type=jnp.float32)).astype(
        jnp.bfloat16
    )
    return (residual + jnp.dot(hidden, down_weight, preferred_element_type=jnp.float32)).astype(
        jnp.bfloat16
    )


def solution(mesh):
    return jax.shard_map(
        shards,
        mesh=mesh,
        in_specs=(
            P(("node", "head"), None),
            P(),
            P(None, "head", None),
            P(),
            P(),
            P(),
            P(),
            P("node", None),
            P("node", None),
        ),
        out_specs=P(("node", "head"), None),
        check_vma=False,
    )
```

```python
import math

import jax
import jax.numpy as jnp
from jax import lax
from jax.experimental import pallas as pl
from jax.experimental.pallas import tpu as pltpu
from jax.sharding import PartitionSpec as P

D = 1024
HD = 64
TILE = 128
NNZ = 8
REACH = 2
WINDOW = 2 * REACH + 1
HALF = 3 * HD // 2
UNROLL = 16
CHUNKS = 8
NEAR = (0, 3, 1, 2)


def layer_norm(values, gain):
    row_mean = jnp.mean(values, -1, keepdims=True)
    centred = values - row_mean
    variance = jnp.mean(centred * centred, -1, keepdims=True)
    return centred * lax.rsqrt(variance + 1e-05) * gain


def project_kernel(
    features_ref, gain_ref, weight_ref, recv_ref,
    weights, normed, outgoing,
    ring_send, ring_recv, swap_send, swap_recv, head_send, head_recv,
):
    heads = weights.shape[0]
    side = math.isqrt(heads)
    me = lax.axis_index("head")
    node = lax.axis_index("node")
    core = lax.rem(node, 2)
    partner = node + 1 - 2 * core
    x = me // side
    y = lax.rem(me, side)
    first = x + core * (y - x)
    second = y + core * (x - y)
    first_stride = side - (side - 1) * core
    second_stride = 1 + (side - 1) * core
    piece = HALF // 2

    def head_of(da, db):
        return (
            lax.rem(first + da % side, side) * first_stride
            + lax.rem(second + db % side, side) * second_stride
        )

    def ring(s, m):
        offset = (0, 0, -1, 0, 0, 1)[m]
        part = (0, 1, 0, 1, 0, 1)[m]
        step = 1 if m < 3 else -1
        if s == 0:
            block, target, own = head_of(offset, 0), head_of(step, 0), offset == 0
        else:
            across = NEAR[s - 1]
            block, target = head_of(across, offset), head_of(0, step)
            own = across == 0 and offset == 0
        there = weights.at[block, core, pl.ds(part * piece, piece)]
        here = weight_ref.at[core, pl.ds(part * piece, piece)] if own else there
        return pltpu.make_async_remote_copy(
            src_ref=here, dst_ref=there,
            send_sem=ring_send.at[s, m], recv_sem=ring_recv.at[s, m],
            device_id={"head": target}, device_id_type=pl.DeviceIdType.MESH,
        )

    def swap(da, db):
        ref = weights.at[head_of(da, db), core]
        slot = (da % side) * first_stride + (db % side) * second_stride
        return pltpu.make_async_remote_copy(
            src_ref=ref, dst_ref=ref, send_sem=swap_send.at[slot], recv_sem=swap_recv.at[slot],
            device_id={"node": partner}, device_id_type=pl.DeviceIdType.MESH,
        )

    def to_head(slot):
        target = lax.rem(x + slot // side, side) * side + lax.rem(y + slot % side, side)
        return pltpu.make_async_remote_copy(
            src_ref=outgoing.at[slot], dst_ref=recv_ref.at[me],
            send_sem=head_send.at[slot], recv_sem=head_recv.at[slot],
            device_id={"head": target}, device_id_type=pl.DeviceIdType.MESH,
        )

    barrier = pltpu.get_barrier_semaphore()
    for k in range(1, heads):
        peer = lax.rem(x + k // side, side) * side + lax.rem(y + k % side, side)
        pl.semaphore_signal(
            barrier, inc=1, device_id={"head": peer}, device_id_type=pl.DeviceIdType.MESH
        )
    pl.semaphore_signal(
        barrier, inc=1, device_id={"node": partner}, device_id_type=pl.DeviceIdType.MESH
    )
    pl.semaphore_wait(barrier, heads)

    def own_sends(s):
        for m in (0, 3, 1, 4):
            ring(s, m).start()

    own_sends(0)
    own_sends(1)

    @pl.loop(0, features_ref.shape[0] // 32)
    def _(i):
        at = pl.ds(pl.multiple_of(i * 32, 32), 32)
        rows = features_ref[at, :].astype(jnp.float32)
        normed[at, :] = layer_norm(rows, gain_ref[...]).astype(jnp.bfloat16)

    rows_half = features_ref.shape[0] // 2

    def project(weight, put):
        result = lax.dot_general(
            normed[...], weight.reshape(2 * HALF, D), (((1,), (1,)), ((), ())),
            preferred_element_type=jnp.float32,
        ).astype(jnp.bfloat16)
        put[: 2 * rows_half, :] = result[:, : 2 * HD]
        put[2 * rows_half :, :] = jnp.concatenate(
            [result[:rows_half, 2 * HD :], result[rows_half:, 2 * HD :]], axis=1
        )

    def project_head(dx, dy):
        slot = dx * side + dy
        block = lax.rem(x + dx, side) * side + lax.rem(y + dy, side)
        other = weights.at[block, 1 - core]
        pltpu.make_async_remote_copy(
            src_ref=other, dst_ref=other, send_sem=swap_send.at[slot], recv_sem=swap_recv.at[slot],
            device_id={"node": partner}, device_id_type=pl.DeviceIdType.MESH,
        ).wait_recv()
        project(weights[block], outgoing.at[slot])
        to_head(slot).start()

    project(weight_ref[...], recv_ref.at[me])

    def near(s):
        ring(s, 0).wait_recv()
        ring(s, 2).start()
        ring(s, 3).wait_recv()
        ring(s, 5).start()
        ring(s, 1).wait_recv()
        ring(s, 4).wait_recv()

    def far(s):
        ring(s, 2).wait_recv()
        ring(s, 5).wait_recv()

    near(0)
    own_sends(2)
    own_sends(3)
    swap(-1, 0).start()
    swap(1, 0).start()
    near(1)
    swap(0, -1).start()
    swap(0, 1).start()
    far(0)
    own_sends(4)
    swap(2, 0).start()
    far(1)
    swap(0, 2).start()

    @pl.loop(0, 4)
    def _(i):
        long = 1 + 2 * lax.rem(i, 2)
        project_head((1 - i // 2) * long, (i // 2) * long)

    near(2)
    swap(-1, -1).start()
    swap(-1, 1).start()
    near(3)
    swap(1, -1).start()
    swap(1, 1).start()

    @pl.loop(0, 2)
    def _(i):
        project_head(2 * (1 - i), 2 * i)

    far(2)
    swap(-1, 2).start()
    far(3)
    swap(1, 2).start()
    near(4)
    swap(2, -1).start()
    swap(2, 1).start()

    @pl.loop(0, 4)
    def _(i):
        project_head(1 + 2 * lax.rem(i, 2), 1 + 2 * (i // 2))

    far(4)
    swap(2, 2).start()

    @pl.loop(0, 4)
    def _(i):
        long = 1 + 2 * lax.rem(i, 2)
        group = i // 2
        project_head((1 - group) * long + 2 * group, 2 * (1 - group) + group * long)

    project_head(2, 2)

    for s in range(5):
        for m in range(6):
            ring(s, m).wait_send()
    for da in range(side):
        for db in range(side):
            if da or db:
                swap(da, db).wait_send()
    for slot in range(1, heads):
        to_head(slot).wait_send()
        to_head(slot).wait_recv()


def project(features, gain, weight):
    heads = lax.axis_size("head")
    rows = features.shape[0]
    vmem = pl.BlockSpec(memory_space=pltpu.VMEM)
    dma = pltpu.SemaphoreType.DMA
    return pl.pallas_call(
        project_kernel,
        out_shape=jax.ShapeDtypeStruct((heads, rows * 3 // 2, 2 * HD), jnp.bfloat16),
        in_specs=[vmem] * 3,
        out_specs=vmem,
        scratch_shapes=[
            pltpu.VMEM((heads, 2, HALF, D), jnp.bfloat16),
            pltpu.VMEM((rows, D), jnp.bfloat16),
            pltpu.VMEM((heads, rows * 3 // 2, 2 * HD), jnp.bfloat16),
            dma((5, 6)),
            dma((5, 6)),
            dma((heads,)),
            dma((heads,)),
            dma((heads,)),
            dma((heads,)),
        ],
        compiler_params=pltpu.CompilerParams(
            collective_id=0, has_side_effects=True, vmem_limit_bytes=40 << 20
        ),
        name="project",
    )(features, gain.reshape(1, D), weight)


def exchange_kernel(
    order_ref, rows_ref, window_ref, query_ref,
    source, reordered, send, recv,
):
    heads = rows_ref.shape[0]
    owned = rows_ref.shape[1] * 2 // 3
    rows = heads * owned
    size = lax.axis_size("node")
    tiles = rows // TILE
    per_chunk = tiles // CHUNKS
    chunk_rows = rows // CHUNKS
    node = lax.axis_index("node")
    core = lax.rem(node, 2)
    partner = node + 1 - 2 * core
    above = lax.rem(node + 2, size)
    below = lax.rem(node + size - 2, size)

    barrier = pltpu.get_barrier_semaphore()
    for peer in (above, below, partner):
        pl.semaphore_signal(
            barrier, inc=1, device_id={"node": peer}, device_id_type=pl.DeviceIdType.MESH
        )

    def flow(f, i):
        source_slot = (REACH, REACH, REACH, 4 - 4 * core)[f]
        target_slot = (0, 2 * REACH, 1 + 2 * core, 3 - 2 * core)[f]
        at = pl.ds(i * per_chunk, per_chunk)
        return pltpu.make_async_remote_copy(
            src_ref=window_ref.at[source_slot, at], dst_ref=window_ref.at[target_slot, at],
            send_sem=send.at[f, i], recv_sem=recv.at[f, i],
            device_id={"node": (above, below, partner, partner)[f]},
            device_id_type=pl.DeviceIdType.MESH,
        )

    @pl.loop(0, heads)
    def _(j):
        at = pl.ds(pl.multiple_of(j * owned, owned), owned)
        source[at, :] = rows_ref[j, :owned].astype(jnp.float32)

    def pick(base):
        @pl.loop(0, chunk_rows // UNROLL)
        def _(b):
            start = pl.multiple_of(base + b * UNROLL, UNROLL)
            for r in range(UNROLL):
                reordered[pl.ds(start + r, 1), :] = source[pl.ds(order_ref[start + r], 1), :]

    pl.semaphore_wait(barrier, 3)

    @pl.loop(0, CHUNKS)
    def _(i):
        pick(i * chunk_rows)
        for k in range(per_chunk):
            tile = i * per_chunk + k
            at = pl.ds(pl.multiple_of(tile * TILE, TILE), TILE)
            window_ref[REACH, tile] = reordered[at, :].astype(jnp.bfloat16)

        @pl.when(i > 0)
        def _():
            for f in range(3):
                flow(f, i - 1).start()

    lane = lax.broadcasted_iota(jnp.int32, (owned // 2, 2 * HD), 1)

    @pl.loop(0, heads)
    def _(j):
        packed = rows_ref[j, owned:].astype(jnp.float32)
        at = pl.multiple_of(j * owned, owned)
        source[pl.ds(at, owned // 2), :] = jnp.where(lane < HD, packed, 0.0)
        source[pl.ds(at + owned // 2, owned // 2), :] = jnp.where(
            lane < HD, pltpu.roll(packed, HD, 1), 0.0
        )

    for f in range(3):
        flow(f, CHUNKS - 1).start()

    def took(f, i):
        at = pl.ds(i * per_chunk, per_chunk)
        pltpu.make_async_remote_copy(
            src_ref=window_ref.at[0, at], dst_ref=window_ref.at[0, at],
            send_sem=send.at[f, i], recv_sem=recv.at[f, i],
            device_id={"node": partner}, device_id_type=pl.DeviceIdType.MESH,
        ).wait_recv()

    @pl.loop(0, CHUNKS)
    def _(i):
        pick(i * chunk_rows)
        for k in range(per_chunk):
            at = pl.ds(pl.multiple_of((i * per_chunk + k) * TILE, TILE), TILE)
            query_ref[at, :] = reordered[at, :].astype(jnp.bfloat16)
        took(1 - core, i)
        flow(3, i).start()

    @pl.loop(0, CHUNKS)
    def _(i):
        took(core, i)
        took(2, i)
        took(3, i)
        for f in range(4):
            flow(f, i).wait_send()


def exchange(order, rows):
    heads = rows.shape[0]
    n = heads * rows.shape[1] * 2 // 3
    vmem = pl.BlockSpec(memory_space=pltpu.VMEM)
    return pl.pallas_call(
        exchange_kernel,
        out_shape=[
            jax.ShapeDtypeStruct((WINDOW, n // TILE, TILE, 2 * HD), jnp.bfloat16),
            jax.ShapeDtypeStruct((n, 2 * HD), jnp.bfloat16),
        ],
        in_specs=[pl.BlockSpec(memory_space=pltpu.SMEM), vmem],
        out_specs=[vmem, vmem],
        scratch_shapes=[
            pltpu.VMEM((n, 2 * HD), jnp.float32),
            pltpu.VMEM((n, 2 * HD), jnp.float32),
            pltpu.SemaphoreType.DMA((4, CHUNKS)),
            pltpu.SemaphoreType.DMA((4, CHUNKS)),
        ],
        compiler_params=pltpu.CompilerParams(
            collective_id=1, has_side_effects=True, vmem_limit_bytes=40 << 20
        ),
        name="exchange",
    )(order, rows)


def attend_tile(t, position_ref, order_ref, query_ref, window, tile_out, restored):
    scale = math.log2(math.e) / math.sqrt(HD)
    query = query_ref[pl.ds(pl.multiple_of(t * TILE, TILE), TILE), :]
    keyval = jnp.concatenate([window[position_ref[t, n]] for n in range(NNZ)], axis=0)
    scores = lax.dot_general(
        query, keyval, (((1,), (1,)), ((), ())), preferred_element_type=jnp.float32
    )
    scores = scores * scale
    expd = jnp.exp2(scores - jnp.max(scores, -1, keepdims=True))
    total = jnp.sum(expd, -1, keepdims=True)
    mixed = jnp.dot(expd.astype(jnp.bfloat16), keyval, preferred_element_type=jnp.float32)
    tile_out[...] = mixed / total
    for r in range(TILE):
        restored[pl.ds(order_ref[t * TILE + r], 1), :] = tile_out[pl.ds(r, 1), :]


def attention_kernel(
    position_ref, order_ref, query_ref, window, out_ref, tile_out, restored
):
    tiles = query_ref.shape[0] // TILE

    @pl.loop(0, tiles)
    def _(t):
        attend_tile(t, position_ref, order_ref, query_ref, window, tile_out, restored)

    @pl.loop(0, tiles)
    def _(t):
        at = pl.ds(pl.multiple_of(t * TILE, TILE), TILE)
        out_ref[at, :] = restored[at, HD:].astype(jnp.bfloat16)


def attention(position, order, query, window):
    n = query.shape[0]
    smem = pl.BlockSpec(memory_space=pltpu.SMEM)
    vmem = pl.BlockSpec(memory_space=pltpu.VMEM)
    return pl.pallas_call(
        attention_kernel,
        out_shape=jax.ShapeDtypeStruct((n, HD), jnp.bfloat16),
        in_specs=[smem, smem, vmem, vmem],
        out_specs=vmem,
        scratch_shapes=[
            pltpu.VMEM((TILE, 2 * HD), jnp.float32),
            pltpu.VMEM((n, 2 * HD), jnp.float32),
        ],
        compiler_params=pltpu.CompilerParams(vmem_limit_bytes=40 << 20),
        name="attention",
    )(position, order, query, window.reshape(WINDOW * n // TILE, TILE, 2 * HD))


def shards(
    features,
    attn_gain,
    qkv_weight,
    out_weight,
    feedforward_norm_gain,
    up_weight,
    down_weight,
    tile_pattern,
    node_order,
):
    own_rows = features.shape[0]
    partitions = lax.axis_size("node")
    rows_part = own_rows * lax.axis_size("head")
    query_tiles = rows_part // TILE
    weight = qkv_weight[:, 0].T
    weight = jnp.concatenate([weight[HD:], weight[:HD]], 0).reshape(2, HALF, D)
    order = node_order[0]
    window, query = exchange(order, project(features, attn_gain, weight))
    partition = lax.axis_index("node")
    position = (
        tile_pattern // query_tiles - partition + REACH + partitions
    ) % partitions * query_tiles + tile_pattern % query_tiles
    restored = attention(position, order, query, window)
    gathered_heads = lax.all_to_all(restored, "head", split_axis=0, concat_axis=1, tiled=True)
    residual = features.astype(jnp.float32) + jnp.dot(
        gathered_heads, out_weight, preferred_element_type=jnp.float32
    )
    mlp_input = layer_norm(residual, feedforward_norm_gain).astype(jnp.bfloat16)
    hidden = jax.nn.gelu(jnp.dot(mlp_input, up_weight, preferred_element_type=jnp.float32)).astype(
        jnp.bfloat16
    )
    return (residual + jnp.dot(hidden, down_weight, preferred_element_type=jnp.float32)).astype(
        jnp.bfloat16
    )


def solution(mesh):
    return jax.shard_map(
        shards,
        mesh=mesh,
        in_specs=(
            P(("node", "head"), None),
            P(),
            P(None, "head", None),
            P(),
            P(),
            P(),
            P(),
            P("node", None),
            P("node", None),
        ),
        out_specs=P(("node", "head"), None),
        check_vma=False,
    )
```

```python
import math

import jax
import jax.numpy as jnp
from jax import lax
from jax.experimental import pallas as pl
from jax.experimental.pallas import tpu as pltpu
from jax.sharding import PartitionSpec as P

D = 1024
HD = 64
TILE = 128
NNZ = 8
REACH = 2
WINDOW = 2 * REACH + 1
HALF = 3 * HD // 2
UNROLL = 16
CHUNKS = 8
NEAR = (0, 3, 1, 2)
TOGETHER = 4
FF_BLOCK = 512


def layer_norm(values, gain):
    row_mean = jnp.mean(values, -1, keepdims=True)
    centred = values - row_mean
    variance = jnp.mean(centred * centred, -1, keepdims=True)
    return centred * lax.rsqrt(variance + 1e-05) * gain


def project_kernel(
    features_ref, gain_ref, weight_ref, recv_ref,
    weights, normed, outgoing,
    ring_send, ring_recv, swap_send, swap_recv, head_send, head_recv,
):
    heads = weights.shape[0]
    side = math.isqrt(heads)
    me = lax.axis_index("head")
    node = lax.axis_index("node")
    core = lax.rem(node, 2)
    partner = node + 1 - 2 * core
    x = me // side
    y = lax.rem(me, side)
    first = x + core * (y - x)
    second = y + core * (x - y)
    first_stride = side - (side - 1) * core
    second_stride = 1 + (side - 1) * core
    piece = HALF // 2

    def head_of(da, db):
        return (
            lax.rem(first + da % side, side) * first_stride
            + lax.rem(second + db % side, side) * second_stride
        )

    def ring(s, m):
        offset = (0, 0, -1, 0, 0, 1)[m]
        part = (0, 1, 0, 1, 0, 1)[m]
        step = 1 if m < 3 else -1
        if s == 0:
            block, target, own = head_of(offset, 0), head_of(step, 0), offset == 0
        else:
            across = NEAR[s - 1]
            block, target = head_of(across, offset), head_of(0, step)
            own = across == 0 and offset == 0
        there = weights.at[block, core, pl.ds(part * piece, piece)]
        here = weight_ref.at[core, pl.ds(part * piece, piece)] if own else there
        return pltpu.make_async_remote_copy(
            src_ref=here, dst_ref=there,
            send_sem=ring_send.at[s, m], recv_sem=ring_recv.at[s, m],
            device_id={"head": target}, device_id_type=pl.DeviceIdType.MESH,
        )

    def swap(da, db):
        ref = weights.at[head_of(da, db), core]
        slot = (da % side) * first_stride + (db % side) * second_stride
        return pltpu.make_async_remote_copy(
            src_ref=ref, dst_ref=ref, send_sem=swap_send.at[slot], recv_sem=swap_recv.at[slot],
            device_id={"node": partner}, device_id_type=pl.DeviceIdType.MESH,
        )

    def to_head(slot):
        target = lax.rem(x + slot // side, side) * side + lax.rem(y + slot % side, side)
        return pltpu.make_async_remote_copy(
            src_ref=outgoing.at[slot], dst_ref=recv_ref.at[me],
            send_sem=head_send.at[slot], recv_sem=head_recv.at[slot],
            device_id={"head": target}, device_id_type=pl.DeviceIdType.MESH,
        )

    barrier = pltpu.get_barrier_semaphore()
    for k in range(1, heads):
        peer = lax.rem(x + k // side, side) * side + lax.rem(y + k % side, side)
        pl.semaphore_signal(
            barrier, inc=1, device_id={"head": peer}, device_id_type=pl.DeviceIdType.MESH
        )
    pl.semaphore_signal(
        barrier, inc=1, device_id={"node": partner}, device_id_type=pl.DeviceIdType.MESH
    )
    pl.semaphore_wait(barrier, heads)

    def own_sends(s):
        for m in (0, 3, 1, 4):
            ring(s, m).start()

    own_sends(0)
    own_sends(1)

    @pl.loop(0, features_ref.shape[0] // 32)
    def _(i):
        at = pl.ds(pl.multiple_of(i * 32, 32), 32)
        rows = features_ref[at, :].astype(jnp.float32)
        normed[at, :] = layer_norm(rows, gain_ref[...]).astype(jnp.bfloat16)

    rows_half = features_ref.shape[0] // 2

    def project(weight, put):
        weight = weight.reshape(2 * HALF, D)
        result = lax.dot_general(
            normed[...], jnp.concatenate([weight[HD:], weight[:HD]], 0), (((1,), (1,)), ((), ())),
            preferred_element_type=jnp.float32,
        ).astype(jnp.bfloat16)
        put[: 2 * rows_half, :] = result[:, : 2 * HD]
        put[2 * rows_half :, :] = jnp.concatenate(
            [result[:rows_half, 2 * HD :], result[rows_half:, 2 * HD :]], axis=1
        )

    def project_head(dx, dy):
        slot = dx * side + dy
        block = lax.rem(x + dx, side) * side + lax.rem(y + dy, side)
        other = weights.at[block, 1 - core]
        pltpu.make_async_remote_copy(
            src_ref=other, dst_ref=other, send_sem=swap_send.at[slot], recv_sem=swap_recv.at[slot],
            device_id={"node": partner}, device_id_type=pl.DeviceIdType.MESH,
        ).wait_recv()
        project(weights[block], outgoing.at[slot])
        to_head(slot).start()

    project(weight_ref[...], recv_ref.at[me])

    def near(s):
        ring(s, 0).wait_recv()
        ring(s, 2).start()
        ring(s, 3).wait_recv()
        ring(s, 5).start()
        ring(s, 1).wait_recv()
        ring(s, 4).wait_recv()

    def far(s):
        ring(s, 2).wait_recv()
        ring(s, 5).wait_recv()

    near(0)
    own_sends(2)
    own_sends(3)
    swap(-1, 0).start()
    swap(1, 0).start()
    near(1)
    swap(0, -1).start()
    swap(0, 1).start()
    far(0)
    own_sends(4)
    swap(2, 0).start()
    far(1)
    swap(0, 2).start()

    @pl.loop(0, 4)
    def _(i):
        long = 1 + 2 * lax.rem(i, 2)
        project_head((1 - i // 2) * long, (i // 2) * long)

    near(2)
    swap(-1, -1).start()
    swap(-1, 1).start()
    near(3)
    swap(1, -1).start()
    swap(1, 1).start()

    @pl.loop(0, 2)
    def _(i):
        project_head(2 * (1 - i), 2 * i)

    far(2)
    swap(-1, 2).start()
    far(3)
    swap(1, 2).start()
    near(4)
    swap(2, -1).start()
    swap(2, 1).start()

    @pl.loop(0, 4)
    def _(i):
        project_head(1 + 2 * lax.rem(i, 2), 1 + 2 * (i // 2))

    far(4)
    swap(2, 2).start()

    @pl.loop(0, 4)
    def _(i):
        long = 1 + 2 * lax.rem(i, 2)
        group = i // 2
        project_head((1 - group) * long + 2 * group, 2 * (1 - group) + group * long)

    project_head(2, 2)

    for s in range(5):
        for m in range(6):
            ring(s, m).wait_send()
    for da in range(side):
        for db in range(side):
            if da or db:
                swap(da, db).wait_send()
    for slot in range(1, heads):
        to_head(slot).wait_send()
        to_head(slot).wait_recv()


def project(features, gain, weight):
    heads = lax.axis_size("head")
    rows = features.shape[0]
    vmem = pl.BlockSpec(memory_space=pltpu.VMEM)
    dma = pltpu.SemaphoreType.DMA
    return pl.pallas_call(
        project_kernel,
        out_shape=jax.ShapeDtypeStruct((heads, rows * 3 // 2, 2 * HD), jnp.bfloat16),
        in_specs=[vmem] * 3,
        out_specs=vmem,
        scratch_shapes=[
            pltpu.VMEM((heads, 2, HALF, D), jnp.bfloat16),
            pltpu.VMEM((rows, D), jnp.bfloat16),
            pltpu.VMEM((heads, rows * 3 // 2, 2 * HD), jnp.bfloat16),
            dma((5, 6)),
            dma((5, 6)),
            dma((heads,)),
            dma((heads,)),
            dma((heads,)),
            dma((heads,)),
        ],
        compiler_params=pltpu.CompilerParams(
            collective_id=0, has_side_effects=True, vmem_limit_bytes=67043328
        ),
        name="project",
    )(features, gain.reshape(1, D), weight)


def exchange_kernel(
    order_ref, rows_ref, window_ref, query_ref,
    source, reordered, send, recv,
):
    heads = rows_ref.shape[0]
    owned = rows_ref.shape[1] * 2 // 3
    rows = heads * owned
    size = lax.axis_size("node")
    tiles = rows // TILE
    per_chunk = tiles // CHUNKS
    chunk_rows = rows // CHUNKS
    node = lax.axis_index("node")
    core = lax.rem(node, 2)
    partner = node + 1 - 2 * core
    above = lax.rem(node + 2, size)
    below = lax.rem(node + size - 2, size)

    barrier = pltpu.get_barrier_semaphore()
    for peer in (above, below, partner):
        pl.semaphore_signal(
            barrier, inc=1, device_id={"node": peer}, device_id_type=pl.DeviceIdType.MESH
        )

    def flow(f, i):
        source_slot = (REACH, REACH, REACH, 4 - 4 * core)[f]
        target_slot = (0, 2 * REACH, 1 + 2 * core, 3 - 2 * core)[f]
        at = pl.ds(i * per_chunk, per_chunk)
        return pltpu.make_async_remote_copy(
            src_ref=window_ref.at[source_slot, at], dst_ref=window_ref.at[target_slot, at],
            send_sem=send.at[f, i], recv_sem=recv.at[f, i],
            device_id={"node": (above, below, partner, partner)[f]},
            device_id_type=pl.DeviceIdType.MESH,
        )

    @pl.loop(0, heads)
    def _(j):
        at = pl.ds(pl.multiple_of(j * owned, owned), owned)
        source[at, :] = rows_ref[j, :owned].astype(jnp.float32)

    def pick(base):
        @pl.loop(0, chunk_rows // UNROLL)
        def _(b):
            start = pl.multiple_of(base + b * UNROLL, UNROLL)
            for r in range(UNROLL):
                reordered[pl.ds(start + r, 1), :] = source[pl.ds(order_ref[start + r], 1), :]

    pl.semaphore_wait(barrier, 3)

    @pl.loop(0, CHUNKS)
    def _(i):
        pick(i * chunk_rows)
        for k in range(per_chunk):
            tile = i * per_chunk + k
            at = pl.ds(pl.multiple_of(tile * TILE, TILE), TILE)
            window_ref[REACH, tile] = reordered[at, :].astype(jnp.bfloat16)

        @pl.when(i > 0)
        def _():
            for f in range(3):
                flow(f, i - 1).start()

    lane = lax.broadcasted_iota(jnp.int32, (owned // 2, 2 * HD), 1)

    @pl.loop(0, heads)
    def _(j):
        packed = rows_ref[j, owned:].astype(jnp.float32)
        at = pl.multiple_of(j * owned, owned)
        source[pl.ds(at, owned // 2), :] = jnp.where(lane < HD, packed, 0.0)
        source[pl.ds(at + owned // 2, owned // 2), :] = jnp.where(
            lane < HD, pltpu.roll(packed, HD, 1), 0.0
        )

    for f in range(3):
        flow(f, CHUNKS - 1).start()

    def took(f, i):
        at = pl.ds(i * per_chunk, per_chunk)
        pltpu.make_async_remote_copy(
            src_ref=window_ref.at[0, at], dst_ref=window_ref.at[0, at],
            send_sem=send.at[f, i], recv_sem=recv.at[f, i],
            device_id={"node": partner}, device_id_type=pl.DeviceIdType.MESH,
        ).wait_recv()

    @pl.loop(0, CHUNKS)
    def _(i):
        pick(i * chunk_rows)
        for k in range(per_chunk):
            at = pl.ds(pl.multiple_of((i * per_chunk + k) * TILE, TILE), TILE)
            query_ref[at, :] = reordered[at, :].astype(jnp.bfloat16)
        took(1 - core, i)
        flow(3, i).start()

    @pl.loop(0, CHUNKS)
    def _(i):
        took(core, i)
        took(2, i)
        took(3, i)
        for f in range(4):
            flow(f, i).wait_send()


def exchange(order, rows):
    heads = rows.shape[0]
    n = heads * rows.shape[1] * 2 // 3
    vmem = pl.BlockSpec(memory_space=pltpu.VMEM)
    return pl.pallas_call(
        exchange_kernel,
        out_shape=[
            jax.ShapeDtypeStruct((WINDOW, n // TILE, TILE, 2 * HD), jnp.bfloat16),
            jax.ShapeDtypeStruct((n, 2 * HD), jnp.bfloat16),
        ],
        in_specs=[pl.BlockSpec(memory_space=pltpu.SMEM), vmem],
        out_specs=[vmem, vmem],
        scratch_shapes=[
            pltpu.VMEM((n, 2 * HD), jnp.float32),
            pltpu.VMEM((n, 2 * HD), jnp.float32),
            pltpu.SemaphoreType.DMA((4, CHUNKS)),
            pltpu.SemaphoreType.DMA((4, CHUNKS)),
        ],
        compiler_params=pltpu.CompilerParams(
            collective_id=1, has_side_effects=True, vmem_limit_bytes=67043328
        ),
        name="exchange",
    )(order, rows)


def attend(tiles, position_ref, order_ref, query_ref, window, tile_out, restored):
    scale = math.log2(math.e) / math.sqrt(HD)
    keyvals, scores = [], []
    for t in tiles:
        query = query_ref[pl.ds(pl.multiple_of(t * TILE, TILE), TILE), :]
        keyval = jnp.concatenate([window[position_ref[t, n]] for n in range(NNZ)], axis=0)
        keyvals.append(keyval)
        scores.append(
            lax.dot_general(
                query, keyval, (((1,), (1,)), ((), ())), preferred_element_type=jnp.float32
            )
        )
    for k, t in enumerate(tiles):
        scaled = scores[k] * scale
        expd = jnp.exp2(scaled - jnp.max(scaled, -1, keepdims=True))
        total = jnp.sum(expd, -1, keepdims=True)
        mixed = jnp.dot(
            expd.astype(jnp.bfloat16), keyvals[k], preferred_element_type=jnp.float32
        )
        tile_out[k] = mixed / total
    for k, t in enumerate(tiles):
        for r in range(TILE):
            restored[pl.ds(order_ref[t * TILE + r], 1), :] = tile_out[k, pl.ds(r, 1), :]


def attention_kernel(
    position_ref, order_ref, query_ref, window, out_ref, tile_out, restored
):
    tiles = query_ref.shape[0] // TILE
    heads, half = out_ref.shape[:2]

    @pl.loop(0, tiles // TOGETHER)
    def _(i):
        attend(
            [i * TOGETHER + k for k in range(TOGETHER)],
            position_ref, order_ref, query_ref, window, tile_out, restored,
        )

    lane = lax.broadcasted_iota(jnp.int32, (half, 2 * HD), 1)

    @pl.loop(0, heads)
    def _(j):
        at = pl.multiple_of(j * 2 * half, 2 * half)
        low = pltpu.roll(restored[pl.ds(at, half), :], HD, 1)
        high = restored[pl.ds(at + half, half), :]
        out_ref[j] = jnp.where(lane < HD, low, high).astype(jnp.bfloat16)


def attention(position, order, query, window, heads):
    n = query.shape[0]
    smem = pl.BlockSpec(memory_space=pltpu.SMEM)
    vmem = pl.BlockSpec(memory_space=pltpu.VMEM)
    return pl.pallas_call(
        attention_kernel,
        out_shape=jax.ShapeDtypeStruct((heads, n // heads // 2, 2 * HD), jnp.bfloat16),
        in_specs=[smem, smem, vmem, vmem],
        out_specs=vmem,
        scratch_shapes=[
            pltpu.VMEM((TOGETHER, TILE, 2 * HD), jnp.float32),
            pltpu.VMEM((n, 2 * HD), jnp.float32),
        ],
        compiler_params=pltpu.CompilerParams(vmem_limit_bytes=67043328),
        name="attention",
    )(position, order, query, window.reshape(WINDOW * n // TILE, TILE, 2 * HD))


def finish_kernel(
    attended_ref, features_ref, gain_ref, out_weight_ref, up_ref, down_ref, updated_ref,
    out_weight, up, down, received, gathered, residual, normed,
    load_sem, send, recv,
):
    heads, half = attended_ref.shape[:2]
    side = math.isqrt(heads)
    me = lax.axis_index("head")
    x = me // side
    y = lax.rem(me, side)
    barrier = pltpu.get_barrier_semaphore()

    def peer(slot):
        return lax.rem(x + slot // side, side) * side + lax.rem(y + slot % side, side)

    for slot in range(1, heads):
        pl.semaphore_signal(
            barrier, inc=1, device_id={"head": peer(slot)}, device_id_type=pl.DeviceIdType.MESH
        )
    loads = [
        pltpu.make_async_copy(a, b, load_sem.at[k])
        for k, (a, b) in enumerate(((out_weight_ref, out_weight), (up_ref, up), (down_ref, down)))
    ]
    for load in loads:
        load.start()
    pl.semaphore_wait(barrier, heads - 1)

    def to_head(slot):
        return pltpu.make_async_remote_copy(
            src_ref=attended_ref.at[peer(slot)], dst_ref=received.at[me],
            send_sem=send.at[slot], recv_sem=recv.at[slot],
            device_id={"head": peer(slot)}, device_id_type=pl.DeviceIdType.MESH,
        )

    for slot in range(1, heads):
        to_head(slot).start()
    received[me] = attended_ref[me]
    for slot in range(1, heads):
        to_head(slot).wait_recv()
    for g in range(heads // 2):
        a, b = received[2 * g], received[2 * g + 1]
        columns = pl.ds(g * 2 * HD, 2 * HD)
        gathered[:half, columns] = jnp.concatenate([a[:, :HD], b[:, :HD]], axis=1)
        gathered[half:, columns] = jnp.concatenate([a[:, HD:], b[:, HD:]], axis=1)
    loads[0].wait()

    @pl.loop(0, D // FF_BLOCK)
    def _(j):
        at = pl.ds(pl.multiple_of(j * FF_BLOCK, FF_BLOCK), FF_BLOCK)
        residual[:, at] = features_ref[:, at].astype(jnp.float32) + jnp.dot(
            gathered[...], out_weight[:, at], preferred_element_type=jnp.float32
        )

    @pl.loop(0, 2 * half // 32)
    def _(i):
        at = pl.ds(pl.multiple_of(i * 32, 32), 32)
        normed[at, :] = layer_norm(residual[at, :], gain_ref[...]).astype(jnp.bfloat16)

    loads[1].wait()
    loads[2].wait()

    @pl.loop(0, up.shape[1] // FF_BLOCK)
    def _(j):
        at = pl.ds(pl.multiple_of(j * FF_BLOCK, FF_BLOCK), FF_BLOCK)
        hidden = jax.nn.gelu(
            jnp.dot(normed[...], up[:, at], preferred_element_type=jnp.float32)
        ).astype(jnp.bfloat16)
        residual[...] += jnp.dot(hidden, down[at, :], preferred_element_type=jnp.float32)

    updated_ref[...] = residual[...].astype(jnp.bfloat16)
    for slot in range(1, heads):
        to_head(slot).wait_send()


def finish(attended, features, gain, out_weight, up, down):
    heads = attended.shape[0]
    rows = features.shape[0]
    vmem = pl.BlockSpec(memory_space=pltpu.VMEM)
    hbm = pl.BlockSpec(memory_space=pl.ANY)
    dma = pltpu.SemaphoreType.DMA
    return pl.pallas_call(
        finish_kernel,
        out_shape=jax.ShapeDtypeStruct((rows, D), jnp.bfloat16),
        in_specs=[vmem, vmem, vmem, hbm, hbm, hbm],
        out_specs=vmem,
        scratch_shapes=[
            pltpu.VMEM(out_weight.shape, jnp.bfloat16),
            pltpu.VMEM(up.shape, jnp.bfloat16),
            pltpu.VMEM(down.shape, jnp.bfloat16),
            pltpu.VMEM(attended.shape, jnp.bfloat16),
            pltpu.VMEM((rows, D), jnp.bfloat16),
            pltpu.VMEM((rows, D), jnp.float32),
            pltpu.VMEM((rows, D), jnp.bfloat16),
            dma((3,)),
            dma((heads,)),
            dma((heads,)),
        ],
        compiler_params=pltpu.CompilerParams(
            collective_id=2, has_side_effects=True, vmem_limit_bytes=67043328
        ),
        name="finish",
    )(attended, features, gain.reshape(1, D), out_weight, up, down)


def shards(
    features,
    attn_gain,
    qkv_weight,
    out_weight,
    feedforward_norm_gain,
    up_weight,
    down_weight,
    tile_pattern,
    node_order,
):
    partitions = lax.axis_size("node")
    heads = lax.axis_size("head")
    query_tiles = features.shape[0] * heads // TILE
    weight = qkv_weight[:, 0].T.reshape(2, HALF, D)
    order = node_order[0]
    window, query = exchange(order, project(features, attn_gain, weight))
    partition = lax.axis_index("node")
    position = (
        tile_pattern // query_tiles - partition + REACH + partitions
    ) % partitions * query_tiles + tile_pattern % query_tiles
    attended = attention(position, order, query, window, heads)
    return finish(attended, features, feedforward_norm_gain, out_weight, up_weight, down_weight)


def solution(mesh):
    return jax.shard_map(
        shards,
        mesh=mesh,
        in_specs=(
            P(("node", "head"), None),
            P(),
            P(None, "head", None),
            P(),
            P(),
            P(),
            P(),
            P("node", None),
            P("node", None),
        ),
        out_specs=P(("node", "head"), None),
        check_vma=False,
    )
```
